32 devices in a mesh: dp: 8 (over z, x), tensor: 4 (over y, core).
Axes of the slice: x: 2, y: 2, z: 4, core: 2. Of those that a mesh axis runs over, the one named last changes fastest.
Arguments:
- frames: bfloat16 [8192, 768], P(('dp', 'tensor')), may hold values from -6 to 6
- w_qkv: bfloat16 [3, 768, 768], P(None, None, 'tensor'), may hold values from -0.21875 to 0.21875
- b_qv: bfloat16 [2, 768], P(None, 'tensor'), may hold values from -3 to 3
- w_out: bfloat16 [768, 768], P('tensor'), may hold values from -4 to 4
- b_out: bfloat16 [768], replicated, may hold values from -3 to 3
- ln1_gain: bfloat16 [768], replicated, may hold values from 0.5 to 1.5
- ln1_bias: bfloat16 [768], replicated, may hold values from -2 to 2
- w_up: bfloat16 [768, 3072], P(None, 'tensor'), may hold values from -0.21875 to 0.21875
- b_up: bfloat16 [3072], P('tensor'), may hold values from -3 to 3
- w_down: bfloat16 [3072, 768], P('tensor'), may hold values from -0.109375 to 0.109375
- b_down: bfloat16 [768], replicated, may hold values from -3 to 3
- ln2_gain: bfloat16 [768], replicated, may hold values from 0.5 to 1.5
- ln2_bias: bfloat16 [768], replicated, may hold values from -2 to 2
- cotangent: bfloat16 [8192, 768], P(('dp', 'tensor')), may hold values from -6 to 6
Outputs:
- mixed: bfloat16 [8192, 768], P(('dp', 'tensor'))
- grad_frames: float32 [8192, 768], P(('dp', 'tensor'))
- grad_w_qkv: float32 [3, 768, 768], P(None, None, 'tensor')
- grad_b_qv: float32 [2, 768], P(None, 'tensor')
- grad_w_out: float32 [768, 768], P('tensor')
- grad_b_out: float32 [768], replicated
- grad_ln1_gain: float32 [768], replicated
- grad_ln1_bias: float32 [768], replicated
- grad_w_up: float32 [768, 3072], P(None, 'tensor')
- grad_b_up: float32 [3072], P('tensor')
- grad_w_down: float32 [3072, 768], P('tensor')
- grad_b_down: float32 [768], replicated
- grad_ln2_gain: float32 [768], replicated
- grad_ln2_bias: float32 [768], replicated
The draws below stay inside these ranges and needn't reach their ends.
All inputs are finite; a program needn't handle non-finite values.
Results may differ from the reference program's by a relative error of at most 0.012.
The reference program's roundings to bfloat16 on the way count: a program that leaves them out, or rounds other values in their place, can miss the bound.
Values may be sent and summed in bfloat16 or wider, within the bound.
No kernel may reach another device: no remote copies, remote signals or barrier semaphores. Data moves between devices by JAX's collectives and lax.ppermute only.
A program may use at most 128 MiB of HBM per device.

```python
import jax
import jax.numpy as jnp
from jax import lax

D = 768
HEADS = 12
HDIM = 64
FF = 3072
SEQ = 1024
CLIPS = 8


def shard_levels(key, extent, cuts, smallest, high):
    gain, own = 1.0, jax.random.fold_in(key, 6)
    for dim, parts in cuts:
        steps = jnp.exp(jax.random.uniform(jax.random.fold_in(own, dim), (parts,), jnp.float32, smallest / len(cuts), high / len(cuts)))
        gain = gain * jnp.repeat(steps, extent[dim] // parts).reshape([-1 if axis == dim else 1 for axis in range(len(extent))])
    return gain


def normal_values(own_key, shape, scale, limit, pieces=(), held_as=jnp.bfloat16):
    values = jax.random.normal(own_key, shape, jnp.float32) * scale
    if len(pieces) > 0:
        values = shard_levels(own_key, shape, pieces, -0.22, 0.18) * values
    return jnp.clip(values, min=-limit, max=limit).astype(held_as)


def setup_inputs(seed: int = 0) -> dict:
    keys = jax.random.split(jax.random.key(seed), 15)
    return {
        "frames": normal_values(keys[0], (CLIPS * SEQ, D), 1.0, 6.0, ((0, 32),)),
        "w_qkv": normal_values(keys[1], (3, D, D), D ** -0.5, 0.21875, ((2, 4),)),
        "b_qv": normal_values(keys[2], (2, D), 0.5, 3.0, ((1, 4),)),
        "w_out": normal_values(keys[3], (D, D), 2 ** -0.5, 4.0, ((0, 4),)),
        "b_out": normal_values(keys[4], (D,), 0.5, 3.0),
        "ln1_gain": jnp.clip(1.0 + 0.1 * jax.random.normal(keys[5], (D,), jnp.float32), 0.5, 1.5).astype(jnp.bfloat16),
        "ln1_bias": normal_values(keys[6], (D,), 0.3, 2.0),
        "w_up": normal_values(keys[7], (D, FF), D ** -0.5, 0.21875, ((1, 4),)),
        "b_up": normal_values(keys[8], (FF,), 0.5, 3.0, ((0, 4),)),
        "w_down": normal_values(keys[9], (FF, D), FF ** -0.5, 0.109375, ((0, 4),)),
        "b_down": normal_values(keys[10], (D,), 0.5, 3.0),
        "ln2_gain": jnp.clip(1.0 + 0.1 * jax.random.normal(keys[11], (D,), jnp.float32), 0.5, 1.5).astype(jnp.bfloat16),
        "ln2_bias": normal_values(keys[12], (D,), 0.3, 2.0),
        "cotangent": normal_values(keys[13], (CLIPS * SEQ, D), 1.0, 6.0, ((0, 32),)),
    }


norm_eps = 1e-05
highest_prec = lax.Precision.HIGHEST

@jax.custom_vjp
def low(v):
    return lax.optimization_barrier(v.astype(jnp.bfloat16)).astype(jnp.float32)

@jax.custom_vjp
def low_back(v):
    return v

def low_keep(v):
    return (low(v), None)

def low_pass(kept, grad):
    return (grad,)

def back_keep(v):
    return (v, None)

def back_low(kept, grad):
    return (low(grad),)
low.defvjp(low_keep, low_pass)
low_back.defvjp(back_keep, back_low)

def matmul(left, right):
    return jnp.dot(left, right, precision=highest_prec, preferred_element_type=jnp.float32)

def normalize(values, gain_vec, shift_vec):
    average = lax.optimization_barrier(jnp.mean(values, axis=-1, keepdims=True))
    centred = values - average
    spread = lax.optimization_barrier(jnp.mean(centred * centred, axis=-1, keepdims=True))
    return centred * lax.rsqrt(spread + norm_eps) * gain_vec + shift_vec

def attend(queries, keys_in, values_in):
    scores = jnp.einsum('qhd,khd->hqk', queries, keys_in, precision=highest_prec) * HDIM ** (-0.5)
    scores = low_back(scores)
    weights = jax.nn.softmax(scores, axis=-1)
    return jnp.einsum('hqk,khd->qhd', low(weights), values_in, precision=highest_prec)

def forward(params, inputs, group):
    w_qkv, b_qv, w_out, b_out, ln1_gain, ln1_bias, w_up, b_up, w_down, b_down, ln2_gain, ln2_bias = params
    normed = low(normalize(inputs, ln1_gain, ln1_bias))
    queries = low(low_back(matmul(normed, w_qkv[0])) + b_qv[0])
    keys_all = low(low_back(matmul(normed, w_qkv[1])))
    values_all = low(low_back(matmul(normed, w_qkv[2])) + b_qv[1])
    shape_heads = (group, SEQ, HEADS, HDIM)
    attended = lax.map(lambda triple: jax.checkpoint(attend)(*triple), (queries.reshape(shape_heads), keys_all.reshape(shape_heads), values_all.reshape(shape_heads)))
    attended = low(low_back(attended.reshape(group * SEQ, D)))
    hidden = inputs + low_back(matmul(attended, w_out)) + b_out
    normed_two = low(normalize(hidden, ln2_gain, ln2_bias))
    pre_act = low_back(matmul(normed_two, w_up)) + b_up
    activated = low(jax.nn.gelu(pre_act, approximate=False))
    return hidden + matmul(activated, w_down) + b_down

def reference(frames, w_qkv, b_qv, w_out, b_out, ln1_gain, ln1_bias, w_up, b_up, w_down, b_down, ln2_gain, ln2_bias, cotangent):
    params = tuple((array_in.astype(jnp.float32) for array_in in (w_qkv, b_qv, w_out, b_out, ln1_gain, ln1_bias, w_up, b_up, w_down, b_down, ln2_gain, ln2_bias)))
    group = 4 if CLIPS % 4 == 0 else 1
    batches = CLIPS // group
    inputs = frames.astype(jnp.float32).reshape(batches, group * SEQ, D)
    cotans = cotangent.astype(jnp.float32).reshape(batches, group * SEQ, D)

    def one_group(totals, pair):
        inputs_group, cotan_group = pair
        result, pullback = jax.vjp(lambda weights, acts: forward(weights, acts, group), params, inputs_group)
        grads, grad_input = pullback(cotan_group)
        totals = jax.tree.map(jnp.add, totals, grads)
        return (totals, (result.astype(jnp.bfloat16), grad_input))
    zeros = jax.tree.map(jnp.zeros_like, params)
    totals, (results, grad_inputs) = lax.scan(one_group, zeros, (inputs, cotans))
    return (results.reshape(CLIPS * SEQ, D), grad_inputs.reshape(CLIPS * SEQ, D), totals[0], totals[1], totals[2], totals[3], totals[4], totals[5], totals[6], totals[7], totals[8], totals[9], totals[10], totals[11])
```

```python
import jax
import jax.numpy as jnp
from jax import lax
from jax.experimental import pallas as pl
from jax.experimental.pallas import tpu as pltpu
from jax.sharding import PartitionSpec as P

HDIM = 64
norm_eps = 1e-05
root_half = 0.7071067811865476
inv_root_tau = 0.3989422804014327
F32 = jnp.float32
BF16 = jnp.bfloat16


def dot(a, b, ca, cb):
    return lax.dot_general(a, b, (((ca,), (cb,)), ((), ())), preferred_element_type=F32)


def normalize(values):
    average = jnp.mean(values, axis=-1, keepdims=True)
    centred = values - average
    inv_std = lax.rsqrt(jnp.mean(centred * centred, axis=-1, keepdims=True) + norm_eps)
    return centred * inv_std, inv_std


def norm_back(upstream, unit_vals, inv_std, gain_vec):
    scaled = upstream * gain_vec
    return inv_std * (
        scaled
        - jnp.mean(scaled, axis=-1, keepdims=True)
        - unit_vals * jnp.mean(scaled * unit_vals, axis=-1, keepdims=True)
    )


def swap(value, axis, size, bit):
    return lax.ppermute(value, axis, [(i, i ^ bit) for i in range(size)])


def near(value):
    return swap(value, "tensor", 4, 1)


def far(value):
    return swap(value, "tensor", 4, 2)


def gather_rows(own):
    across = far(own)
    beside = near(own)
    corner = near(across)
    return own, beside, across, corner


def scatter_rows(own, beside, across, corner):
    passed = across + near(corner.astype(BF16)).astype(F32)
    passed = far(passed.astype(BF16))
    return own + near(beside.astype(BF16)).astype(F32) + passed.astype(F32)


def sum_over_clips(grad, size, bits):
    index = lax.axis_index("dp")
    held = grad
    for bit in bits:
        half = held.shape[0] // 2
        upper = (index & bit) != 0
        send = lax.dynamic_slice_in_dim(held, jnp.where(upper, 0, half), half, 0)
        keep = lax.dynamic_slice_in_dim(held, jnp.where(upper, half, 0), half, 0)
        got = swap(send, "dp", size, bit)
        held = (keep.astype(F32) + got.astype(F32)).astype(BF16)
    for bit in reversed(bits):
        upper = (index & bit) != 0
        got = swap(held, "dp", size, bit)
        held = jnp.concatenate(
            [jnp.where(upper, got, held), jnp.where(upper, held, got)], axis=0
        )
    return held


def sum_small(values, size, bits):
    for bit in bits:
        values = values + swap(values, "dp", size, bit)
    return values


def attend_kernel(q_ref, k_ref, v_ref, o_ref, lse_ref):
    heads = q_ref.shape[1] // HDIM
    for h in range(heads):
        cols = slice(h * HDIM, (h + 1) * HDIM)
        q = q_ref[:, cols] * (HDIM**-0.5)
        scores = dot(q, k_ref[:, cols], 1, 1)
        peak = jnp.max(scores, axis=-1, keepdims=True)
        exponent = jnp.exp(scores - peak)
        totals = jnp.sum(exponent, axis=-1, keepdims=True)
        weights = (exponent * (1.0 / totals)).astype(BF16)
        o_ref[:, cols] = dot(weights, v_ref[:, cols], 1, 0).astype(BF16)
        lse_ref[:, h : h + 1] = peak + jnp.log(totals)


def attend(q, k, v):
    rows, width = q.shape
    block = rows // 4
    row_spec = pl.BlockSpec((block, width), lambda i: (i, 0))
    full = pl.BlockSpec((rows, width), lambda i: (0, 0))
    heads = width // HDIM
    return pl.pallas_call(
        attend_kernel,
        grid=(4,),
        in_specs=[row_spec, full, full],
        out_specs=[row_spec, pl.BlockSpec((block, heads), lambda i: (i, 0))],
        out_shape=[
            jax.ShapeDtypeStruct((rows, width), BF16),
            jax.ShapeDtypeStruct((rows, heads), F32),
        ],
        cost_estimate=pl.CostEstimate(
            flops=4 * rows * rows * width,
            bytes_accessed=8 * rows * width,
            transcendentals=rows * rows * heads,
        ),
        name="attend",
    )(q, k, v)


def attend_back_kernel(
    q_ref, k_ref, v_ref, g_ref, lse_ref, dq_ref, dk_ref, dv_ref, sums_ref, acc_k, acc_v
):
    step = pl.program_id(0)
    heads = q_ref.shape[1] // HDIM

    @pl.when(step == 0)
    def _():
        acc_k[...] = jnp.zeros_like(acc_k)
        acc_v[...] = jnp.zeros_like(acc_v)
        sums_ref[...] = jnp.zeros_like(sums_ref)

    for h in range(heads):
        cols = slice(h * HDIM, (h + 1) * HDIM)
        q = q_ref[:, cols] * (HDIM**-0.5)
        k = k_ref[:, cols]
        g = g_ref[:, cols]
        probs = jnp.exp(dot(q, k, 1, 1) - lse_ref[:, h : h + 1])
        grad_probs = dot(g, v_ref[:, cols], 1, 1)
        inner = jnp.sum(probs * grad_probs, axis=-1, keepdims=True)
        grad_scores = (probs * (grad_probs - inner)).astype(BF16)
        grad_q = dot(grad_scores, k, 1, 0) * (HDIM**-0.5)
        dq_ref[:, cols] = grad_q.astype(BF16)
        sums_ref[0:1, cols] += jnp.sum(grad_q, axis=0, keepdims=True)
        acc_k[cols, :] += dot(q, grad_scores, 0, 0)
        acc_v[cols, :] += dot(g, probs.astype(BF16), 0, 0)

    @pl.when(step == pl.num_programs(0) - 1)
    def _():
        dk_ref[...] = acc_k[...].T.astype(BF16)
        grad_v = acc_v[...].T
        dv_ref[...] = grad_v.astype(BF16)
        sums_ref[1:2, :] = jnp.sum(grad_v, axis=0, keepdims=True)


def attend_back(q, k, v, grad, lse):
    rows, width = q.shape
    block = rows // 4
    row_spec = pl.BlockSpec((block, width), lambda i: (i, 0))
    full = pl.BlockSpec((rows, width), lambda i: (0, 0))
    heads = width // HDIM
    return pl.pallas_call(
        attend_back_kernel,
        grid=(4,),
        in_specs=[row_spec, full, full, row_spec, pl.BlockSpec((block, heads), lambda i: (i, 0))],
        out_specs=[row_spec, full, full, pl.BlockSpec((8, width), lambda i: (0, 0))],
        out_shape=[jax.ShapeDtypeStruct((rows, width), BF16)] * 3
        + [jax.ShapeDtypeStruct((8, width), F32)],
        scratch_shapes=[pltpu.VMEM((width, rows), F32)] * 2,
        cost_estimate=pl.CostEstimate(
            flops=10 * rows * rows * width,
            bytes_accessed=16 * rows * width,
            transcendentals=rows * rows * heads,
        ),
        name="attend_back",
    )(q, k, v, grad, lse)


def on_device(
    clips,
    frames,
    w_qkv,
    b_qv,
    w_out,
    b_out,
    ln1_gain,
    ln1_bias,
    w_up,
    b_up,
    w_down,
    b_down,
    ln2_gain,
    ln2_bias,
    cotangent,
):
    bits = [1 << i for i in range(clips.bit_length() - 1)]
    late = bits[1:] + bits[:1]
    gain_one = ln1_gain.astype(F32)
    shift_one = ln1_bias.astype(F32)
    gain_two = ln2_gain.astype(F32)
    shift_two = ln2_bias.astype(F32)
    own_rows = frames.shape[0]

    frames_all = jnp.concatenate(gather_rows(frames), axis=0)
    grad_all = jnp.concatenate(gather_rows(cotangent), axis=0)

    inputs_all = frames_all.astype(F32)
    unit_one, inv_one = normalize(inputs_all)
    normed = (unit_one * gain_one + shift_one).astype(BF16)
    bias_qv = b_qv.astype(F32)
    queries = (dot(normed, w_qkv[0], 1, 0) + bias_qv[0]).astype(BF16)
    keys_all = dot(normed, w_qkv[1], 1, 0).astype(BF16)
    values_all = (dot(normed, w_qkv[2], 1, 0) + bias_qv[1]).astype(BF16)
    attended, lse = attend(queries, keys_all, values_all)

    half = 2 * own_rows
    second = dot(attended[half:], w_out, 1, 0)
    first = dot(attended[:half], w_out, 1, 0)
    projected = scatter_rows(first[:own_rows], first[own_rows:], second[:own_rows], second[own_rows:])
    hidden = frames.astype(F32) + projected + b_out.astype(F32)
    unit_two, inv_two = normalize(hidden)
    normed_two = jnp.concatenate(
        gather_rows((unit_two * gain_two + shift_two).astype(BF16)), axis=0
    )

    grad_act = dot(grad_all, w_down, 1, 1)
    pre_act = dot(normed_two, w_up, 1, 0) + b_up.astype(F32)
    phi = 0.5 * (1.0 + lax.erf(pre_act * root_half))
    activated = (pre_act * phi).astype(BF16)
    grad_pre = grad_act * (phi + pre_act * inv_root_tau * jnp.exp(-0.5 * pre_act * pre_act))
    grad_b_up = jnp.sum(grad_pre, axis=0)
    grad_pre = grad_pre.astype(BF16)

    second = dot(grad_pre[half:], w_up, 1, 1)
    first = dot(grad_pre[:half], w_up, 1, 1)
    grad_norm_two = scatter_rows(
        first[:own_rows], first[own_rows:], second[:own_rows], second[own_rows:]
    )
    grad_w_down = sum_over_clips(dot(activated, grad_all, 0, 0).astype(BF16), clips, bits)
    grad_w_up = sum_over_clips(dot(normed_two, grad_pre, 0, 0).astype(BF16), clips, bits)

    upstream = cotangent.astype(F32)
    grad_hidden = upstream + norm_back(grad_norm_two, unit_two, inv_two, gain_two)
    grad_hidden_all = jnp.concatenate(gather_rows(grad_hidden.astype(BF16)), axis=0)

    second = dot(activated[half:], w_down, 1, 0)
    first = dot(activated[:half], w_down, 1, 0)
    mixed = (
        hidden
        + scatter_rows(first[:own_rows], first[own_rows:], second[:own_rows], second[own_rows:])
        + b_down.astype(F32)
    ).astype(BF16)

    grad_att = dot(grad_hidden_all, w_out, 1, 1).astype(BF16)
    grad_w_out = sum_over_clips(dot(attended, grad_hidden_all, 0, 0).astype(BF16), clips, bits)
    grad_q, grad_k, grad_v, qv_sums = attend_back(queries, keys_all, values_all, grad_att, lse)
    grad_proj = jnp.concatenate([grad_q, grad_k, grad_v], axis=1)
    w_all = jnp.concatenate([w_qkv[0], w_qkv[1], w_qkv[2]], axis=1)
    grad_w_qkv = sum_over_clips(dot(normed, grad_proj, 0, 0).astype(BF16), clips, late)
    partial = dot(grad_proj, w_all, 1, 1)
    grad_norm_one = scatter_rows(
        partial[:own_rows],
        partial[own_rows:half],
        partial[half : half + own_rows],
        partial[half + own_rows :],
    )
    grad_frames = grad_hidden + norm_back(
        grad_norm_one, unit_one[:own_rows], inv_one[:own_rows], gain_one
    )
    shared = jnp.stack(
        [
            jnp.sum(partial * unit_one, axis=0),
            jnp.sum(partial, axis=0),
            jnp.sum(grad_norm_two * unit_two, axis=0),
            jnp.sum(grad_norm_two, axis=0),
            jnp.sum(grad_hidden, axis=0),
            jnp.sum(upstream, axis=0),
        ]
    )
    shared = shared + near(shared)
    shared = shared + far(shared)
    width = shared.shape[1]
    split = qv_sums.shape[1]
    own_sums = jnp.stack([grad_b_up, jnp.pad(qv_sums[:2].reshape(-1), (0, width - 2 * split))])
    sums = sum_small(jnp.concatenate([shared, own_sums], axis=0), clips, bits)
    grad_w_qkv = jnp.stack(
        [grad_w_qkv[:, j * split : (j + 1) * split] for j in range(3)]
    ).astype(F32)
    return (
        mixed,
        grad_frames,
        grad_w_qkv,
        sums[7, : 2 * split].reshape(2, split),
        grad_w_out.astype(F32),
        sums[4],
        sums[0],
        sums[1],
        grad_w_up.astype(F32),
        sums[6],
        grad_w_down.astype(F32),
        sums[5],
        sums[2],
        sums[3],
    )


def solution(mesh):
    def body(*args):
        return on_device(mesh.shape["dp"], *args)

    rows = P(("dp", "tensor"), None)
    return jax.shard_map(
        body,
        mesh=mesh,
        in_specs=(
            rows,
            P(None, None, "tensor"),
            P(None, "tensor"),
            P("tensor", None),
            P(),
            P(),
            P(),
            P(None, "tensor"),
            P("tensor"),
            P("tensor", None),
            P(),
            P(),
            P(),
            rows,
        ),
        out_specs=(
            rows,
            rows,
            P(None, None, "tensor"),
            P(None, "tensor"),
            P("tensor", None),
            P(),
            P(),
            P(),
            P(None, "tensor"),
            P("tensor"),
            P("tensor", None),
            P(),
            P(),
            P(),
        ),
        check_vma=False,
    )
```
